32 devices in a mesh: groups: 2 (over y), req: 4 (over z), head: 2 (over x), pair: 2 (over core).
Axes of the slice: x: 2, y: 2, z: 4, core: 2. Of those that a mesh axis runs over, the one named last changes fastest.
Arguments:
- query: bfloat16 [256, 8192], P(('groups', 'req', 'pair'), 'head'), parts along dimension 0, may hold values from -80 to 80
- new_keys: bfloat16 [256, 512], P(('groups', 'req', 'pair'), 'head'), parts along dimension 0, may hold values from -4 to 4
- new_values: bfloat16 [256, 512], P(('groups', 'req', 'pair'), 'head'), parts along dimension 0, may hold values from -4 to 4
- key_cache: bfloat16 [256, 512, 512], P(('groups', 'req', 'pair'), None, 'head'), parts along dimension 0, may hold values from -4 to 4
- value_cache: bfloat16 [256, 512, 512], P(('groups', 'req', 'pair'), None, 'head'), parts along dimension 0, may hold values from -4 to 4
- lengths: int32 [256], P(('groups', 'req', 'pair')), parts along dimension 0, may hold values from 1 to 512, as said below
- residual: bfloat16 [256, 8192], P(('groups', 'req', 'pair'), 'head'), parts along dimension 0, may hold values from -1.6 to 1.6
- norm_gain: float32 [8192], P('head'), may hold values from 0.5 to 1.5
- gate_weight: bfloat16 [26624, 8192], P(('req', 'pair'), 'head'), may hold values from -0.0625 to 0.0625
- up_weight: bfloat16 [26624, 8192], P(('req', 'pair'), 'head'), may hold values from -0.0625 to 0.0625
- down_weight: bfloat16 [26624, 8192], P(('req', 'pair'), 'head'), may hold values from -0.0390625 to 0.0390625
Outputs:
- mixed: bfloat16 [256, 8192], P(('groups', 'req', 'pair'), 'head'), parts along dimension 0
The draws below stay inside these ranges and needn't reach their ends.
There are 2 independent parts, one for each index of `groups`. The reference program is written for one: setup_inputs(seed, part) draws one part's arguments, and reference() takes and returns one part's arrays. A program takes and returns all parts, laid end to end along the dimension named above; an argument that names none is the same for every part. Nothing has to cross between parts.
Inputs may be any that keep to these rules, and one draw needn't show every extreme that they name: `lengths`: every row has at least one cached position in use; in every draw some row uses all 512.
All inputs are finite; a program needn't handle non-finite values.
Results may differ from the reference program's by a relative error of at most 0.023.
Values may be sent and summed in bfloat16 or wider, within the bound.
A program may use at most 192 MiB of HBM per device.

```python
import math
import jax
import jax.numpy as jnp
from jax import lax

HEAD_DIM = 128
HEADS = 64
KV_HEADS = 4
GROUP = 16
D = 8192
FF = 26624
CACHE = 512
SLOT_DEV = 16
SLOTS = 128


def shared_keys(key):
    shared = jax.random.normal(jax.random.fold_in(key, 101), (SLOTS, KV_HEADS * HEAD_DIM), jnp.float32)
    return jnp.clip(shared, -4.0, 4.0)


def draw_new_keys(key, part):
    return shared_keys(key).astype(jnp.bfloat16)


def draw_query(key, part):
    result = jnp.clip(jax.random.normal(jax.random.fold_in(key, 1), (SLOTS, HEADS, HEAD_DIM), jnp.float32), -4.0, 4.0)
    return result.reshape(SLOTS, HEADS * HEAD_DIM).astype(jnp.bfloat16)


def draw_key_cache(key, part):
    full_shape = (SLOTS, CACHE, KV_HEADS * HEAD_DIM)
    result = jnp.clip(jax.random.normal(jax.random.fold_in(key, 1), full_shape, jnp.float32), -4.0, 4.0)
    return result.astype(jnp.bfloat16)


def draw_residual(key, part):
    columns = jnp.arange(D, dtype=jnp.float32) / D
    entries = jnp.clip(jax.random.normal(jax.random.fold_in(key, 1), (SLOTS, D), jnp.float32), -4.0, 4.0)
    result = 0.1 * entries * jnp.sqrt(1.0 + 2.0 * columns)[None, :]
    return result.astype(jnp.bfloat16)


def draw_lengths(key, part):
    devices_count = SLOTS // SLOT_DEV
    limits = jax.random.randint(jax.random.fold_in(key, 1), (devices_count, 1), CACHE // 4, CACHE + 1)
    raw_bits = jax.random.randint(jax.random.fold_in(key, 2), (devices_count, SLOT_DEV), 0, 1 << 20)
    picked = (1 + raw_bits % limits).reshape(SLOTS)
    target = jax.random.randint(jax.random.fold_in(key, 3), (), 0, SLOTS)
    return picked.at[target].set(CACHE).astype(jnp.int32)


def steps_of(stream_key, extent, cuts, smallest, largest):
    def one(axis_at, shards_of):
        draws = jax.random.uniform(jax.random.fold_in(jax.random.fold_in(stream_key, 6), axis_at), (shards_of,), jnp.float32, smallest / len(cuts), largest / len(cuts))
        return jnp.repeat(jnp.exp(draws), extent[axis_at] // shards_of).reshape((-1,) + (1,) * (len(extent) - axis_at - 1))

    factor_of = one(*cuts[0])
    for cut in cuts[1:]:
        factor_of = factor_of * one(*cut)
    return factor_of


def scatter_about(key, extent, deviation, reach, pieces=(), kind=jnp.bfloat16):
    values = jax.random.normal(key, extent, jnp.float32) * deviation
    if len(pieces) > 0:
        values = steps_of(key, extent, pieces, -0.22, 0.18) * values
    return jnp.clip(values, min=-reach, max=reach).astype(kind)


def setup_inputs(seed: int = 0, part: int = 0) -> dict:
    splits = jax.random.split(jax.random.key(seed), 12)
    own_keys = jax.random.split(jax.random.fold_in(splits[11], part), 12)
    query = draw_query(jax.random.fold_in(jax.random.fold_in(splits[11], part), 71), part)
    new_keys = draw_new_keys(jax.random.fold_in(jax.random.fold_in(splits[11], part), 71), part)
    new_values = scatter_about(own_keys[2], (SLOTS, KV_HEADS * HEAD_DIM), 1.0, 4.0, ((0, 8), (1, 2)))
    key_cache = draw_key_cache(jax.random.fold_in(jax.random.fold_in(splits[11], part), 71), part)
    value_cache = scatter_about(own_keys[4], (SLOTS, CACHE, KV_HEADS * HEAD_DIM), 1.0, 4.0, ((0, 8), (2, 2)))
    lengths = draw_lengths(jax.random.fold_in(jax.random.fold_in(splits[11], part), 71), part)
    residual = draw_residual(jax.random.fold_in(jax.random.fold_in(splits[11], part), 71), part)
    norm_gain = jnp.clip(1.0 + 0.1 * jax.random.normal(splits[7], (D,), jnp.float32), 0.5, 1.5)
    gate_weight = scatter_about(splits[8], (FF, D), D ** -0.5, 0.0625, ((0, 8), (1, 2)))
    up_weight = scatter_about(splits[9], (FF, D), D ** -0.5, 0.0625, ((0, 8), (1, 2)))
    down_weight = scatter_about(splits[10], (FF, D), FF ** -0.5, 0.0390625, ((0, 8), (1, 2)))
    return {"query": query, "new_keys": new_keys, "new_values": new_values, "key_cache": key_cache, "value_cache": value_cache, "lengths": lengths, "residual": residual, "norm_gain": norm_gain, "gate_weight": gate_weight, "up_weight": up_weight, "down_weight": down_weight}


highest = lax.Precision.HIGHEST
contract_last = (((1,), (1,)), ((), ()))

def attend_row(inputs):
    query_row, key_new, value_new, key_rows, value_rows, length = inputs
    query_heads = query_row.astype(jnp.float32).reshape(KV_HEADS, GROUP, HEAD_DIM)
    key_heads = key_rows.astype(jnp.float32).reshape(CACHE, KV_HEADS, HEAD_DIM)
    value_heads = value_rows.astype(jnp.float32).reshape(CACHE, KV_HEADS, HEAD_DIM)
    own_key = key_new.astype(jnp.float32).reshape(KV_HEADS, HEAD_DIM)
    own_value = value_new.astype(jnp.float32).reshape(KV_HEADS, HEAD_DIM)
    score_scale = 1.0 / math.sqrt(HEAD_DIM)
    scores = jnp.einsum('gjd,tgd->gjt', query_heads, key_heads, precision=highest) * score_scale
    own_score = jnp.einsum('gjd,gd->gj', query_heads, own_key, precision=highest) * score_scale
    is_live = (jnp.arange(CACHE) < length)[None, None, :]
    row_max = jnp.maximum(lax.optimization_barrier(jnp.max(jnp.where(is_live, scores, -jnp.inf), axis=2)), own_score)
    weights = jnp.where(is_live, jnp.exp(scores - row_max[:, :, None]), 0.0)
    own_weight = jnp.exp(own_score - row_max)
    weight_sum = lax.optimization_barrier(jnp.sum(weights, axis=2)) + own_weight
    summed = jnp.einsum('gjt,tgd->gjd', weights, value_heads, precision=highest)
    summed = summed + own_weight[:, :, None] * own_value[:, None, :]
    return (summed / weight_sum[:, :, None]).reshape(HEADS * HEAD_DIM)

def reference(query, new_keys, new_values, key_cache, value_cache, lengths, residual, norm_gain, gate_weight, up_weight, down_weight):
    attention = lax.map(attend_row, (query, new_keys, new_values, key_cache, value_cache, lengths))
    stream = residual.astype(jnp.float32) + attention
    mean_square = lax.optimization_barrier(jnp.mean(stream * stream, axis=1, keepdims=True))
    normed = (stream * lax.rsqrt(mean_square + 1e-05) * norm_gain).astype(jnp.bfloat16)
    gate_out = lax.dot_general(normed, gate_weight, contract_last, preferred_element_type=jnp.float32)
    up_out = lax.dot_general(normed, up_weight, contract_last, preferred_element_type=jnp.float32)
    hidden = (jax.nn.silu(gate_out) * up_out).astype(jnp.bfloat16)
    ffn_out = jnp.dot(hidden, down_weight, preferred_element_type=jnp.float32)
    return (stream + ffn_out).astype(jnp.bfloat16)
```

```python
import functools
import math

import jax
import jax.numpy as jnp
from jax import lax
from jax.experimental import pallas as pl
from jax.experimental.pallas import tpu as pltpu
from jax.sharding import PartitionSpec as P

HEAD_DIM = 128
GROUP = 16
D = 8192
CACHE = 512


highest = lax.Precision.HIGHEST
contract_last = (((1,), (1,)), ((), ()))
low_value = -1e30


MESH = pl.DeviceIdType.MESH
HIDDEN_LAG = 3
DOWN_LAG = 6
SLOT_BYTES = 40 * 2**20


def block_kernel(
    sizes,
    stream_ref, gain_ref, gate_hbm, up_hbm, down_hbm, out_ref,
    wbuf, ssum, xg, tf, pb, precv, hid, acc, psd, prv, zs, zr,
    wsem, ss_send, ss_recv, ag_send, ag_recv, agp_send, agp_recv,
    rs_send, rs_recv, hg_send, hg_recv, pr_send, pr_recv, z_send, z_recv,
):
    reqs, heads, chunks, unit, slots, rows, feats, total_feats = sizes
    block = reqs * 2 * rows
    part = block // heads
    my_req = lax.axis_index("req")
    my_head = lax.axis_index("head")
    my_pair = lax.axis_index("pair")
    other = 1 - my_pair
    head_peers = [lax.rem(my_head + d, heads) for d in range(1, heads)]
    req_peers = [lax.rem(my_req + d, reqs) for d in range(1, reqs)]
    loads = 3 * chunks

    def remote(src, dst, send, recv, device):
        return pltpu.make_async_remote_copy(
            src_ref=src, dst_ref=dst, send_sem=send, recv_sem=recv,
            device_id=device, device_id_type=MESH,
        )

    def load_of(hbm, chunk, slot):
        return pltpu.make_async_copy(
            hbm.at[pl.ds(pl.multiple_of(chunk * unit, unit), unit)], wbuf.at[slot], wsem.at[slot]
        )

    for j in range(min(slots, loads)):
        if j < 2 * chunks:
            load_of(up_hbm if j % 2 else gate_hbm, j // 2, j).start()
        else:
            load_of(down_hbm, j - 2 * chunks, j).start()

    barrier = pltpu.get_barrier_semaphore()
    for peer in head_peers:
        pl.semaphore_signal(barrier, inc=1, device_id={"head": peer}, device_id_type=MESH)
    for peer in req_peers:
        pl.semaphore_signal(barrier, inc=1, device_id={"req": peer}, device_id_type=MESH)
    pl.semaphore_signal(barrier, inc=1, device_id={"pair": other}, device_id_type=MESH)
    pl.semaphore_wait(barrier, heads + reqs - 1)

    stream = stream_ref[...]
    squares = jnp.sum(stream * stream, axis=1, keepdims=True)
    ssum[my_head] = jnp.broadcast_to(squares, (rows, HEAD_DIM))

    def square_copy(owner, peer):
        return remote(ssum.at[owner], ssum.at[owner], ss_send.at[peer], ss_recv.at[owner], {"head": peer})

    for peer in head_peers:
        square_copy(my_head, peer).start()
    for peer in head_peers:
        square_copy(peer, peer).wait_recv()
    mean = jnp.sum(ssum[...], axis=0)[:, :1] / total_feats
    xg[my_req, my_pair] = (stream * lax.rsqrt(mean + 1e-05) * gain_ref[...]).astype(jnp.bfloat16)

    def gather_copy(owner, peer):
        here = xg.at[owner, my_pair]
        return remote(here, here, ag_send.at[peer], ag_recv.at[owner], {"req": peer})

    def pair_copy(owner, side):
        here = xg.at[owner, side]
        return remote(here, here, agp_send.at[owner], agp_recv.at[owner], {"pair": other})

    for peer in reversed(req_peers):
        gather_copy(my_req, peer).start()
    pair_copy(my_req, my_pair).start()
    for peer in req_peers:
        gather_copy(peer, peer).wait_recv()
        pair_copy(peer, my_pair).start()
    for owner in [my_req] + req_peers:
        pair_copy(owner, other).wait_recv()

    acc[...] = jnp.zeros_like(acc)

    def sum_copy(chunk, owner, peer):
        return remote(
            pb.at[chunk, peer], precv.at[chunk, owner],
            rs_send.at[chunk, peer], rs_recv.at[chunk, owner], {"head": peer},
        )

    def hidden_copy(chunk, owner, peer):
        here = hid.at[chunk, owner]
        return remote(here, here, hg_send.at[chunk, peer], hg_recv.at[chunk, owner], {"head": peer})

    def step(t, carry):
        @pl.when(t < chunks)
        def _():
            for side, hbm in enumerate((gate_hbm, up_hbm)):
                slot = lax.rem(2 * t + side, slots)
                load_of(hbm, t, slot).wait()
                x = xg[...].reshape(block, feats)
                sums = lax.dot_general(
                    x, wbuf[slot], contract_last, preferred_element_type=jnp.float32
                ).reshape(heads, part, unit)
                tf[t, :, side] = sums
                pb[t, :, side] = sums.astype(jnp.bfloat16)
            for peer in head_peers:
                sum_copy(t, my_head, peer).start()
            for side in range(2):
                later = slots + 2 * t + side
                slot = lax.rem(later, slots)

                @pl.when(later < 2 * chunks)
                def _():
                    load_of((gate_hbm, up_hbm)[side], later // 2, slot).start()

                @pl.when((later >= 2 * chunks) & (later < loads))
                def _():
                    load_of(down_hbm, later - 2 * chunks, slot).start()

        @pl.when((t >= HIDDEN_LAG) & (t < chunks + HIDDEN_LAG))
        def _():
            k = t - HIDDEN_LAG
            gate = tf[k, my_head, 0]
            up = tf[k, my_head, 1]
            for peer in head_peers:
                sum_copy(k, peer, peer).wait_recv()
                gate = gate + precv[k, peer, 0].astype(jnp.float32)
                up = up + precv[k, peer, 1].astype(jnp.float32)
            hid[k, my_head] = (jax.nn.silu(gate) * up).astype(jnp.bfloat16)
            for peer in head_peers:
                hidden_copy(k, my_head, peer).start()

        @pl.when(t >= DOWN_LAG)
        def _():
            k = t - DOWN_LAG
            slot = lax.rem(2 * chunks + k, slots)
            load_of(down_hbm, k, slot).wait()
            for peer in head_peers:
                hidden_copy(k, peer, peer).wait_recv()
            h = hid[k].reshape(block, unit)
            tile = 512
            for c in range(0, feats, tile):
                d = jnp.dot(h, wbuf[slot, :, c : c + tile], preferred_element_type=jnp.float32)
                acc[:, :, :, c : c + tile] += d.reshape(reqs, 2, rows, tile)
            for peer in head_peers:
                sum_copy(k, my_head, peer).wait_send()
                hidden_copy(k, my_head, peer).wait_send()

        return carry

    lax.fori_loop(0, chunks + DOWN_LAG, step, 0)

    def swap_copy(owner):
        return remote(psd.at[owner], prv.at[owner], pr_send.at[owner], pr_recv.at[owner], {"pair": other})

    def total_copy(owner, peer):
        return remote(zs.at[peer], zr.at[owner], z_send.at[peer], z_recv.at[owner], {"req": peer})

    order = list(reversed(req_peers)) + [my_req]
    for owner in order:
        psd[owner] = acc[owner, other].astype(jnp.bfloat16)
        swap_copy(owner).start()
    for peer in order[:-1]:
        swap_copy(peer).wait_recv()
        zs[peer] = (acc[peer, my_pair] + prv[peer].astype(jnp.float32)).astype(jnp.bfloat16)
        total_copy(my_req, peer).start()
    swap_copy(my_req).wait_recv()
    result = stream_ref[...] + acc[my_req, my_pair] + prv[my_req].astype(jnp.float32)
    for peer in req_peers:
        total_copy(peer, peer).wait_recv()
        result = result + zr[peer].astype(jnp.float32)
    out_ref[...] = result.astype(jnp.bfloat16)

    for peer in head_peers:
        square_copy(my_head, peer).wait_send()
    for peer in req_peers:
        gather_copy(my_req, peer).wait_send()
        total_copy(my_req, peer).wait_send()
    for owner in order:
        pair_copy(owner, my_pair).wait_send()
        swap_copy(owner).wait_send()


def feed_forward(reqs, heads, stream, norm_gain, gate_weight, up_weight, down_weight):
    rows, feats = stream.shape
    units = gate_weight.shape[0]
    unit = max(u for u in range(16, 257, 16) if units % u == 0)
    chunks = units // unit
    slots = min(3 * chunks, SLOT_BYTES // (unit * feats * 2) // 2 * 2)
    block = reqs * 2 * rows
    part = block // heads
    sizes = (reqs, heads, chunks, unit, slots, rows, feats, D)
    bf16, f32 = jnp.bfloat16, jnp.float32
    dma = pltpu.SemaphoreType.DMA
    vmem = pl.BlockSpec(memory_space=pltpu.VMEM)
    hbm = pl.BlockSpec(memory_space=pl.ANY)
    return pl.pallas_call(
        functools.partial(block_kernel, sizes),
        out_shape=jax.ShapeDtypeStruct((rows, feats), bf16),
        in_specs=[vmem, vmem, hbm, hbm, hbm],
        out_specs=vmem,
        scratch_shapes=[
            pltpu.VMEM((slots, unit, feats), bf16),
            pltpu.VMEM((heads, rows, HEAD_DIM), f32),
            pltpu.VMEM((reqs, 2, rows, feats), bf16),
            pltpu.VMEM((chunks, heads, 2, part, unit), f32),
            pltpu.VMEM((chunks, heads, 2, part, unit), bf16),
            pltpu.VMEM((chunks, heads, 2, part, unit), bf16),
            pltpu.VMEM((chunks, heads, part, unit), bf16),
            pltpu.VMEM((reqs, 2, rows, feats), f32),
            pltpu.VMEM((reqs, rows, feats), bf16),
            pltpu.VMEM((reqs, rows, feats), bf16),
            pltpu.VMEM((reqs, rows, feats), bf16),
            pltpu.VMEM((reqs, rows, feats), bf16),
            dma((slots,)),
            dma((heads,)), dma((heads,)),
            dma((reqs,)), dma((reqs,)), dma((reqs,)), dma((reqs,)),
            dma((chunks, heads)), dma((chunks, heads)), dma((chunks, heads)), dma((chunks, heads)),
            dma((reqs,)), dma((reqs,)), dma((reqs,)), dma((reqs,)),
        ],
        compiler_params=pltpu.CompilerParams(
            collective_id=0, has_side_effects=True, vmem_limit_bytes=66_000_000
        ),
    )(stream, norm_gain.reshape(1, feats), gate_weight, up_weight, down_weight)


def local(
    reqs,
    heads,
    query,
    new_keys,
    new_values,
    key_cache,
    value_cache,
    lengths,
    residual,
    norm_gain,
    gate_weight,
    up_weight,
    down_weight,
):
    slot_rows = query.shape[0]
    local_kv = new_keys.shape[1] // HEAD_DIM
    score_scale = 1.0 / math.sqrt(HEAD_DIM)
    query_heads = query.reshape(slot_rows, local_kv, GROUP, HEAD_DIM)
    key_heads = key_cache.reshape(slot_rows, CACHE, local_kv, HEAD_DIM)
    scores = (
        jnp.einsum("sgjd,stgd->sgjt", query_heads, key_heads, preferred_element_type=jnp.float32)
        * score_scale
    )
    own_score = (
        jnp.einsum(
            "sgjd,sgd->sgj",
            query_heads,
            new_keys.reshape(slot_rows, local_kv, HEAD_DIM),
            preferred_element_type=jnp.float32,
        )
        * score_scale
    )
    is_live = lax.broadcasted_iota(jnp.int32, (slot_rows, CACHE), 1) < lengths[:, None]
    live_mask = is_live[:, None, None, :]
    row_max = jnp.maximum(jnp.max(jnp.where(live_mask, scores, low_value), axis=3), own_score)
    weights = jnp.where(live_mask, jnp.exp(scores - row_max[..., None]), 0.0)
    own_weight = jnp.exp(own_score - row_max)
    weight_sum = jnp.sum(weights, axis=3) + own_weight
    value_heads = value_cache.reshape(slot_rows, CACHE, local_kv, HEAD_DIM).astype(jnp.float32)
    summed = jnp.einsum("sgjt,stgd->sgjd", weights, value_heads, precision=highest)
    summed = summed + own_weight[..., None] * new_values.reshape(
        slot_rows, local_kv, 1, HEAD_DIM
    ).astype(jnp.float32)
    attention = (summed / weight_sum[..., None]).reshape(slot_rows, local_kv * GROUP * HEAD_DIM)
    stream = residual.astype(jnp.float32) + attention
    return feed_forward(reqs, heads, stream, norm_gain, gate_weight, up_weight, down_weight)


def solution(mesh):
    return jax.shard_map(
        functools.partial(local, mesh.shape["req"], mesh.shape["head"]),
        mesh=mesh,
        in_specs=(
            P(("groups", "req", "pair"), "head"),
            P(("groups", "req", "pair"), "head"),
            P(("groups", "req", "pair"), "head"),
            P(("groups", "req", "pair"), None, "head"),
            P(("groups", "req", "pair"), None, "head"),
            P(("groups", "req", "pair")),
            P(("groups", "req", "pair"), "head"),
            P("head"),
            P(("req", "pair"), "head"),
            P(("req", "pair"), "head"),
            P(("req", "pair"), "head"),
        ),
        out_specs=P(("groups", "req", "pair"), "head"),
        check_vma=False,
    )
```

```python
import functools
import math

import jax
import jax.numpy as jnp
from jax import lax
from jax.experimental import pallas as pl
from jax.experimental.pallas import tpu as pltpu
from jax.sharding import PartitionSpec as P

HEAD_DIM = 128
GROUP = 16
D = 8192
CACHE = 512


highest = lax.Precision.HIGHEST
low_value = -1e30


MESH = pl.DeviceIdType.MESH
HIDDEN_LAG = 2
DOWN_LAG = 4
SLOT_BYTES = 40 * 2**20


def block_kernel(
    sizes,
    stream_ref, gain_ref, gate_hbm, up_hbm, down_hbm, out_ref,
    wbuf, ssum, xg, xt, tf, pb, precv, hid, acc, psd, prv, zs, zr,
    wsem, ss_send, ss_recv, ag_send, ag_recv, agp_send, agp_recv,
    rs_send, rs_recv, hg_send, hg_recv, pr_send, pr_recv, z_send, z_recv,
):
    reqs, heads, chunks, unit, slots, rows, feats, total_feats = sizes
    block = reqs * 2 * rows
    part = unit // heads
    my_req = lax.axis_index("req")
    my_head = lax.axis_index("head")
    my_pair = lax.axis_index("pair")
    other = 1 - my_pair
    head_peers = [lax.rem(my_head + d, heads) for d in range(1, heads)]
    req_peers = [lax.rem(my_req + d, reqs) for d in range(1, reqs)]
    loads = 3 * chunks

    def remote(src, dst, send, recv, device):
        return pltpu.make_async_remote_copy(
            src_ref=src, dst_ref=dst, send_sem=send, recv_sem=recv,
            device_id=device, device_id_type=MESH,
        )

    def load_of(hbm, chunk, slot):
        return pltpu.make_async_copy(
            hbm.at[pl.ds(pl.multiple_of(chunk * unit, unit), unit)], wbuf.at[slot], wsem.at[slot]
        )

    for j in range(min(slots, loads)):
        if j < 2 * chunks:
            load_of(up_hbm if j % 2 else gate_hbm, j // 2, j).start()
        else:
            load_of(down_hbm, j - 2 * chunks, j).start()

    barrier = pltpu.get_barrier_semaphore()
    for peer in head_peers:
        pl.semaphore_signal(barrier, inc=1, device_id={"head": peer}, device_id_type=MESH)
    for peer in req_peers:
        pl.semaphore_signal(barrier, inc=1, device_id={"req": peer}, device_id_type=MESH)
    pl.semaphore_signal(barrier, inc=1, device_id={"pair": other}, device_id_type=MESH)
    pl.semaphore_wait(barrier, heads + reqs - 1)

    stream = stream_ref[...]
    squares = jnp.sum(stream * stream, axis=1, keepdims=True)
    ssum[my_head] = jnp.broadcast_to(squares, (rows, HEAD_DIM))

    def square_copy(owner, peer):
        return remote(ssum.at[owner], ssum.at[owner], ss_send.at[peer], ss_recv.at[owner], {"head": peer})

    for peer in head_peers:
        square_copy(my_head, peer).start()
    for peer in head_peers:
        square_copy(peer, peer).wait_recv()
    mean = jnp.sum(ssum[...], axis=0)[:, :1] / total_feats
    xg[my_req, my_pair] = (stream * lax.rsqrt(mean + 1e-05) * gain_ref[...]).astype(jnp.bfloat16)

    def gather_copy(owner, peer):
        here = xg.at[owner, my_pair]
        return remote(here, here, ag_send.at[peer], ag_recv.at[owner], {"req": peer})

    def pair_copy(owner, side):
        here = xg.at[owner, side]
        return remote(here, here, agp_send.at[owner], agp_recv.at[owner], {"pair": other})

    for peer in reversed(req_peers):
        gather_copy(my_req, peer).start()
    pair_copy(my_req, my_pair).start()
    for peer in req_peers:
        gather_copy(peer, peer).wait_recv()
        pair_copy(peer, my_pair).start()
    for owner in [my_req] + req_peers:
        pair_copy(owner, other).wait_recv()

    acc[...] = jnp.zeros_like(acc)
    for c in range(0, feats, 512):
        xt[c : c + 512, :] = xg[:, :, :, c : c + 512].reshape(block, 512).T

    def sum_copy(chunk, owner, peer):
        return remote(
            pb.at[chunk, peer], precv.at[chunk, owner],
            rs_send.at[chunk, peer], rs_recv.at[chunk, owner], {"head": peer},
        )

    def hidden_copy(chunk, owner, peer):
        here = hid.at[chunk, owner]
        return remote(here, here, hg_send.at[chunk, peer], hg_recv.at[chunk, owner], {"head": peer})

    def step(t, carry):
        @pl.when(t < chunks)
        def _():
            for side, hbm in enumerate((gate_hbm, up_hbm)):
                slot = lax.rem(2 * t + side, slots)
                load_of(hbm, t, slot).wait()
                sums = jnp.dot(
                    wbuf[slot], xt[...], preferred_element_type=jnp.float32
                ).reshape(heads, part, block)
                tf[t, :, side] = sums
                pb[t, :, side] = sums.astype(jnp.bfloat16)
            for peer in head_peers:
                sum_copy(t, my_head, peer).start()
            for side in range(2):
                later = slots + 2 * t + side
                slot = lax.rem(later, slots)

                @pl.when(later < 2 * chunks)
                def _():
                    load_of((gate_hbm, up_hbm)[side], later // 2, slot).start()

                @pl.when((later >= 2 * chunks) & (later < loads))
                def _():
                    load_of(down_hbm, later - 2 * chunks, slot).start()

        @pl.when((t >= HIDDEN_LAG) & (t < chunks + HIDDEN_LAG))
        def _():
            k = t - HIDDEN_LAG
            gate = tf[k, my_head, 0]
            up = tf[k, my_head, 1]
            for peer in head_peers:
                sum_copy(k, peer, peer).wait_recv()
                gate = gate + precv[k, peer, 0].astype(jnp.float32)
                up = up + precv[k, peer, 1].astype(jnp.float32)
            hid[k, my_head] = (jax.nn.silu(gate) * up).astype(jnp.bfloat16)
            for peer in head_peers:
                hidden_copy(k, my_head, peer).start()

        @pl.when(t >= DOWN_LAG)
        def _():
            k = t - DOWN_LAG
            slot = lax.rem(2 * chunks + k, slots)
            load_of(down_hbm, k, slot).wait()
            for peer in head_peers:
                hidden_copy(k, peer, peer).wait_recv()
            h = hid[k].reshape(unit, block).T
            tile = 512
            for c in range(0, feats, tile):
                d = jnp.dot(h, wbuf[slot, :, c : c + tile], preferred_element_type=jnp.float32)
                acc[:, :, :, c : c + tile] += d.reshape(reqs, 2, rows, tile)
            for peer in head_peers:
                sum_copy(k, my_head, peer).wait_send()
                hidden_copy(k, my_head, peer).wait_send()

        return carry

    lax.fori_loop(0, chunks + DOWN_LAG, step, 0)

    def swap_copy(owner):
        return remote(psd.at[owner], prv.at[owner], pr_send.at[owner], pr_recv.at[owner], {"pair": other})

    def total_copy(owner, peer):
        return remote(zs.at[peer], zr.at[owner], z_send.at[peer], z_recv.at[owner], {"req": peer})

    order = list(reversed(req_peers)) + [my_req]
    for owner in order:
        psd[owner] = acc[owner, other].astype(jnp.bfloat16)
        swap_copy(owner).start()
    for peer in order[:-1]:
        swap_copy(peer).wait_recv()
        zs[peer] = (acc[peer, my_pair] + prv[peer].astype(jnp.float32)).astype(jnp.bfloat16)
        total_copy(my_req, peer).start()
    swap_copy(my_req).wait_recv()
    result = stream_ref[...] + acc[my_req, my_pair] + prv[my_req].astype(jnp.float32)
    for peer in req_peers:
        total_copy(peer, peer).wait_recv()
        result = result + zr[peer].astype(jnp.float32)
    out_ref[...] = result.astype(jnp.bfloat16)

    for peer in head_peers:
        square_copy(my_head, peer).wait_send()
    for peer in req_peers:
        gather_copy(my_req, peer).wait_send()
        total_copy(my_req, peer).wait_send()
    for owner in order:
        pair_copy(owner, my_pair).wait_send()
        swap_copy(owner).wait_send()


def feed_forward(reqs, heads, stream, norm_gain, gate_weight, up_weight, down_weight):
    rows, feats = stream.shape
    units = gate_weight.shape[0]
    unit = max(u for u in range(16 * heads, 257, 16 * heads) if units % u == 0)
    chunks = units // unit
    slots = min(3 * chunks, SLOT_BYTES // (unit * feats * 2) // 2 * 2)
    block = reqs * 2 * rows
    part = unit // heads
    sizes = (reqs, heads, chunks, unit, slots, rows, feats, D)
    bf16, f32 = jnp.bfloat16, jnp.float32
    dma = pltpu.SemaphoreType.DMA
    vmem = pl.BlockSpec(memory_space=pltpu.VMEM)
    hbm = pl.BlockSpec(memory_space=pl.ANY)
    return pl.pallas_call(
        functools.partial(block_kernel, sizes),
        out_shape=jax.ShapeDtypeStruct((rows, feats), bf16),
        in_specs=[vmem, vmem, hbm, hbm, hbm],
        out_specs=vmem,
        scratch_shapes=[
            pltpu.VMEM((slots, unit, feats), bf16),
            pltpu.VMEM((heads, rows, HEAD_DIM), f32),
            pltpu.VMEM((reqs, 2, rows, feats), bf16),
            pltpu.VMEM((feats, block), bf16),
            pltpu.VMEM((chunks, heads, 2, part, block), f32),
            pltpu.VMEM((chunks, heads, 2, part, block), bf16),
            pltpu.VMEM((chunks, heads, 2, part, block), bf16),
            pltpu.VMEM((chunks, heads, part, block), bf16),
            pltpu.VMEM((reqs, 2, rows, feats), f32),
            pltpu.VMEM((reqs, rows, feats), bf16),
            pltpu.VMEM((reqs, rows, feats), bf16),
            pltpu.VMEM((reqs, rows, feats), bf16),
            pltpu.VMEM((reqs, rows, feats), bf16),
            dma((slots,)),
            dma((heads,)), dma((heads,)),
            dma((reqs,)), dma((reqs,)), dma((reqs,)), dma((reqs,)),
            dma((chunks, heads)), dma((chunks, heads)), dma((chunks, heads)), dma((chunks, heads)),
            dma((reqs,)), dma((reqs,)), dma((reqs,)), dma((reqs,)),
        ],
        compiler_params=pltpu.CompilerParams(
            collective_id=0, has_side_effects=True, vmem_limit_bytes=66_000_000
        ),
    )(stream, norm_gain.reshape(1, feats), gate_weight, up_weight, down_weight)


def local(
    reqs,
    heads,
    query,
    new_keys,
    new_values,
    key_cache,
    value_cache,
    lengths,
    residual,
    norm_gain,
    gate_weight,
    up_weight,
    down_weight,
):
    slot_rows = query.shape[0]
    local_kv = new_keys.shape[1] // HEAD_DIM
    score_scale = 1.0 / math.sqrt(HEAD_DIM)
    query_heads = query.reshape(slot_rows, local_kv, GROUP, HEAD_DIM)
    key_heads = key_cache.reshape(slot_rows, CACHE, local_kv, HEAD_DIM)
    scores = (
        jnp.einsum("sgjd,stgd->sgjt", query_heads, key_heads, preferred_element_type=jnp.float32)
        * score_scale
    )
    own_score = (
        jnp.einsum(
            "sgjd,sgd->sgj",
            query_heads,
            new_keys.reshape(slot_rows, local_kv, HEAD_DIM),
            preferred_element_type=jnp.float32,
        )
        * score_scale
    )
    is_live = lax.broadcasted_iota(jnp.int32, (slot_rows, CACHE), 1) < lengths[:, None]
    live_mask = is_live[:, None, None, :]
    row_max = jnp.maximum(jnp.max(jnp.where(live_mask, scores, low_value), axis=3), own_score)
    weights = jnp.where(live_mask, jnp.exp(scores - row_max[..., None]), 0.0)
    own_weight = jnp.exp(own_score - row_max)
    weight_sum = jnp.sum(weights, axis=3) + own_weight
    value_heads = value_cache.reshape(slot_rows, CACHE, local_kv, HEAD_DIM).astype(jnp.float32)
    summed = jnp.einsum("sgjt,stgd->sgjd", weights, value_heads, precision=highest)
    summed = summed + own_weight[..., None] * new_values.reshape(
        slot_rows, local_kv, 1, HEAD_DIM
    ).astype(jnp.float32)
    attention = (summed / weight_sum[..., None]).reshape(slot_rows, local_kv * GROUP * HEAD_DIM)
    stream = residual.astype(jnp.float32) + attention
    return feed_forward(reqs, heads, stream, norm_gain, gate_weight, up_weight, down_weight)


def solution(mesh):
    return jax.shard_map(
        functools.partial(local, mesh.shape["req"], mesh.shape["head"]),
        mesh=mesh,
        in_specs=(
            P(("groups", "req", "pair"), "head"),
            P(("groups", "req", "pair"), "head"),
            P(("groups", "req", "pair"), "head"),
            P(("groups", "req", "pair"), None, "head"),
            P(("groups", "req", "pair"), None, "head"),
            P(("groups", "req", "pair")),
            P(("groups", "req", "pair"), "head"),
            P("head"),
            P(("req", "pair"), "head"),
            P(("req", "pair"), "head"),
            P(("req", "pair"), "head"),
        ),
        out_specs=P(("groups", "req", "pair"), "head"),
        check_vma=False,
    )
```

```python
import functools
import math

import jax
import jax.numpy as jnp
from jax import lax
from jax.experimental import pallas as pl
from jax.experimental.pallas import tpu as pltpu
from jax.sharding import PartitionSpec as P

HEAD_DIM = 128
GROUP = 16
D = 8192
CACHE = 512


highest = lax.Precision.HIGHEST
low_value = -1e30


MESH = pl.DeviceIdType.MESH
HIDDEN_LAG = 1
DOWN_LAG = 3
SLOT_BYTES = 40 * 2**20


def block_kernel(
    sizes,
    stream_ref, gain_ref, gate_hbm, up_hbm, down_hbm, out_ref,
    wbuf, ssum, xg, xt, tf, pb, precv, hid, acc, psd, prv, zs, zr,
    wsem, ss_send, ss_recv, ag_send, ag_recv, agp_send, agp_recv,
    rs_send, rs_recv, hg_send, hg_recv, pr_send, pr_recv, z_send, z_recv,
):
    reqs, heads, chunks, unit, slots, rows, feats, total_feats = sizes
    block = reqs * 2 * rows
    part = unit // heads
    my_req = lax.axis_index("req")
    my_head = lax.axis_index("head")
    my_pair = lax.axis_index("pair")
    other = 1 - my_pair
    head_peers = [lax.rem(my_head + d, heads) for d in range(1, heads)]
    req_peers = [lax.rem(my_req + d, reqs) for d in range(1, reqs)]
    loads = 3 * chunks

    def remote(src, dst, send, recv, device):
        return pltpu.make_async_remote_copy(
            src_ref=src, dst_ref=dst, send_sem=send, recv_sem=recv,
            device_id=device, device_id_type=MESH,
        )

    def load_of(hbm, chunk, slot):
        return pltpu.make_async_copy(
            hbm.at[pl.ds(pl.multiple_of(chunk * unit, unit), unit)], wbuf.at[slot], wsem.at[slot]
        )

    for j in range(min(slots, loads)):
        if j < 2 * chunks:
            load_of(up_hbm if j % 2 else gate_hbm, j // 2, j).start()
        else:
            load_of(down_hbm, j - 2 * chunks, j).start()

    barrier = pltpu.get_barrier_semaphore()
    for peer in head_peers:
        pl.semaphore_signal(barrier, inc=1, device_id={"head": peer}, device_id_type=MESH)
    for peer in req_peers:
        pl.semaphore_signal(barrier, inc=1, device_id={"req": peer}, device_id_type=MESH)
    pl.semaphore_signal(barrier, inc=1, device_id={"pair": other}, device_id_type=MESH)
    pl.semaphore_wait(barrier, heads + reqs - 1)

    stream = stream_ref[...]
    squares = jnp.sum(stream * stream, axis=1, keepdims=True)
    ssum[my_head] = jnp.broadcast_to(squares, (rows, HEAD_DIM))

    def square_copy(owner, peer):
        return remote(ssum.at[owner], ssum.at[owner], ss_send.at[peer], ss_recv.at[owner], {"head": peer})

    for peer in head_peers:
        square_copy(my_head, peer).start()
    for peer in head_peers:
        square_copy(peer, peer).wait_recv()
    mean = jnp.sum(ssum[...], axis=0)[:, :1] / total_feats
    xg[my_req, my_pair] = (stream * lax.rsqrt(mean + 1e-05) * gain_ref[...]).astype(jnp.bfloat16)

    def gather_copy(owner, peer):
        here = xg.at[owner, my_pair]
        return remote(here, here, ag_send.at[peer], ag_recv.at[owner], {"req": peer})

    def pair_copy(owner, side):
        here = xg.at[owner, side]
        return remote(here, here, agp_send.at[owner], agp_recv.at[owner], {"pair": other})

    for peer in reversed(req_peers):
        gather_copy(my_req, peer).start()
    pair_copy(my_req, my_pair).start()
    for peer in req_peers:
        gather_copy(peer, peer).wait_recv()
        pair_copy(peer, my_pair).start()
    for owner in [my_req] + req_peers:
        pair_copy(owner, other).wait_recv()

    acc[...] = jnp.zeros_like(acc)
    for c in range(0, feats, 512):
        xt[c : c + 512, :] = xg[:, :, :, c : c + 512].reshape(block, 512).T

    def sum_copy(chunk, owner, peer):
        return remote(
            pb.at[chunk, peer], precv.at[chunk, owner],
            rs_send.at[chunk, peer], rs_recv.at[chunk, owner], {"head": peer},
        )

    def hidden_copy(chunk, owner, peer):
        here = hid.at[chunk, owner]
        return remote(here, here, hg_send.at[chunk, peer], hg_recv.at[chunk, owner], {"head": peer})

    def step(t, carry):
        @pl.when(t < chunks)
        def _():
            for side, hbm in enumerate((gate_hbm, up_hbm)):
                slot = lax.rem(2 * t + side, slots)
                load_of(hbm, t, slot).wait()
                sums = jnp.dot(
                    wbuf[slot], xt[...], preferred_element_type=jnp.float32
                ).reshape(heads, part, block)
                tf[t, :, side] = sums
                pb[t, :, side] = sums.astype(jnp.bfloat16)
            for peer in head_peers:
                sum_copy(t, my_head, peer).start()
            for side in range(2):
                later = slots + 2 * t + side
                slot = lax.rem(later, slots)

                @pl.when(later < 2 * chunks)
                def _():
                    load_of((gate_hbm, up_hbm)[side], later // 2, slot).start()

                @pl.when((later >= 2 * chunks) & (later < loads))
                def _():
                    load_of(down_hbm, later - 2 * chunks, slot).start()

        @pl.when((t >= HIDDEN_LAG) & (t < chunks + HIDDEN_LAG))
        def _():
            k = t - HIDDEN_LAG
            gate = tf[k, my_head, 0]
            up = tf[k, my_head, 1]
            for peer in head_peers:
                sum_copy(k, peer, peer).wait_recv()
                gate = gate + precv[k, peer, 0].astype(jnp.float32)
                up = up + precv[k, peer, 1].astype(jnp.float32)
            hid[k, my_head] = (jax.nn.silu(gate) * up).astype(jnp.bfloat16)
            for peer in head_peers:
                hidden_copy(k, my_head, peer).start()

        @pl.when(t >= DOWN_LAG)
        def _():
            k = t - DOWN_LAG
            slot = lax.rem(2 * chunks + k, slots)
            load_of(down_hbm, k, slot).wait()
            for peer in head_peers:
                hidden_copy(k, peer, peer).wait_recv()
            h = hid[k].reshape(unit, block).T
            tile = 512
            for c in range(0, feats, tile):
                d = jnp.dot(h, wbuf[slot, :, c : c + tile], preferred_element_type=jnp.float32)
                acc[:, :, :, c : c + tile] += d.reshape(reqs, 2, rows, tile)
            for peer in head_peers:
                sum_copy(k, my_head, peer).wait_send()
                hidden_copy(k, my_head, peer).wait_send()

        return carry

    lax.fori_loop(0, chunks + DOWN_LAG, step, 0)

    def swap_copy(owner):
        return remote(psd.at[owner], prv.at[owner], pr_send.at[owner], pr_recv.at[owner], {"pair": other})

    def total_copy(owner, peer):
        return remote(zs.at[peer], zr.at[owner], z_send.at[peer], z_recv.at[owner], {"req": peer})

    order = list(reversed(req_peers)) + [my_req]
    for owner in order:
        psd[owner] = acc[owner, other].astype(jnp.bfloat16)
        swap_copy(owner).start()
    for peer in order[:-1]:
        swap_copy(peer).wait_recv()
        zs[peer] = (acc[peer, my_pair] + prv[peer].astype(jnp.float32)).astype(jnp.bfloat16)
        total_copy(my_req, peer).start()
    swap_copy(my_req).wait_recv()
    result = stream_ref[...] + acc[my_req, my_pair] + prv[my_req].astype(jnp.float32)
    for peer in req_peers:
        total_copy(peer, peer).wait_recv()
        result = result + zr[peer].astype(jnp.float32)
    out_ref[...] = result.astype(jnp.bfloat16)

    for peer in head_peers:
        square_copy(my_head, peer).wait_send()
    for peer in req_peers:
        gather_copy(my_req, peer).wait_send()
        total_copy(my_req, peer).wait_send()
    for owner in order:
        pair_copy(owner, my_pair).wait_send()
        swap_copy(owner).wait_send()


def feed_forward(reqs, heads, stream, norm_gain, gate_weight, up_weight, down_weight):
    rows, feats = stream.shape
    units = gate_weight.shape[0]
    unit = max(u for u in range(16 * heads, 257, 16 * heads) if units % u == 0)
    chunks = units // unit
    slots = min(3 * chunks, SLOT_BYTES // (unit * feats * 2) // 2 * 2)
    block = reqs * 2 * rows
    part = unit // heads
    sizes = (reqs, heads, chunks, unit, slots, rows, feats, D)
    bf16, f32 = jnp.bfloat16, jnp.float32
    dma = pltpu.SemaphoreType.DMA
    vmem = pl.BlockSpec(memory_space=pltpu.VMEM)
    hbm = pl.BlockSpec(memory_space=pl.ANY)
    return pl.pallas_call(
        functools.partial(block_kernel, sizes),
        out_shape=jax.ShapeDtypeStruct((rows, feats), bf16),
        in_specs=[vmem, vmem, hbm, hbm, hbm],
        out_specs=vmem,
        scratch_shapes=[
            pltpu.VMEM((slots, unit, feats), bf16),
            pltpu.VMEM((heads, rows, HEAD_DIM), f32),
            pltpu.VMEM((reqs, 2, rows, feats), bf16),
            pltpu.VMEM((feats, block), bf16),
            pltpu.VMEM((chunks, heads, 2, part, block), f32),
            pltpu.VMEM((chunks, heads, 2, part, block), bf16),
            pltpu.VMEM((chunks, heads, 2, part, block), bf16),
            pltpu.VMEM((chunks, heads, part, block), bf16),
            pltpu.VMEM((reqs, 2, rows, feats), f32),
            pltpu.VMEM((reqs, rows, feats), bf16),
            pltpu.VMEM((reqs, rows, feats), bf16),
            pltpu.VMEM((reqs, rows, feats), bf16),
            pltpu.VMEM((reqs, rows, feats), bf16),
            dma((slots,)),
            dma((heads,)), dma((heads,)),
            dma((reqs,)), dma((reqs,)), dma((reqs,)), dma((reqs,)),
            dma((chunks, heads)), dma((chunks, heads)), dma((chunks, heads)), dma((chunks, heads)),
            dma((reqs,)), dma((reqs,)), dma((reqs,)), dma((reqs,)),
        ],
        compiler_params=pltpu.CompilerParams(
            collective_id=0, has_side_effects=True, vmem_limit_bytes=66_000_000
        ),
    )(stream, norm_gain.reshape(1, feats), gate_weight, up_weight, down_weight)


def local(
    reqs,
    heads,
    query,
    new_keys,
    new_values,
    key_cache,
    value_cache,
    lengths,
    residual,
    norm_gain,
    gate_weight,
    up_weight,
    down_weight,
):
    slot_rows = query.shape[0]
    local_kv = new_keys.shape[1] // HEAD_DIM
    score_scale = 1.0 / math.sqrt(HEAD_DIM)
    query_heads = query.reshape(slot_rows, local_kv, GROUP, HEAD_DIM)
    key_heads = key_cache.reshape(slot_rows, CACHE, local_kv, HEAD_DIM)
    scores = (
        jnp.einsum("sgjd,stgd->sgjt", query_heads, key_heads, preferred_element_type=jnp.float32)
        * score_scale
    )
    own_score = (
        jnp.einsum(
            "sgjd,sgd->sgj",
            query_heads,
            new_keys.reshape(slot_rows, local_kv, HEAD_DIM),
            preferred_element_type=jnp.float32,
        )
        * score_scale
    )
    is_live = lax.broadcasted_iota(jnp.int32, (slot_rows, CACHE), 1) < lengths[:, None]
    live_mask = is_live[:, None, None, :]
    row_max = jnp.maximum(jnp.max(jnp.where(live_mask, scores, low_value), axis=3), own_score)
    weights = jnp.where(live_mask, jnp.exp(scores - row_max[..., None]), 0.0)
    own_weight = jnp.exp(own_score - row_max)
    weight_sum = jnp.sum(weights, axis=3) + own_weight
    value_heads = value_cache.reshape(slot_rows, CACHE, local_kv, HEAD_DIM).astype(jnp.float32)
    summed = jnp.einsum("sgjt,stgd->sgjd", weights, value_heads, precision=highest)
    summed = summed + own_weight[..., None] * new_values.reshape(
        slot_rows, local_kv, 1, HEAD_DIM
    ).astype(jnp.float32)
    attention = (summed / weight_sum[..., None]).reshape(slot_rows, local_kv * GROUP * HEAD_DIM)
    stream = residual.astype(jnp.float32) + attention
    return feed_forward(reqs, heads, stream, norm_gain, gate_weight, up_weight, down_weight)


def solution(mesh):
    return jax.shard_map(
        functools.partial(local, mesh.shape["req"], mesh.shape["head"]),
        mesh=mesh,
        in_specs=(
            P(("groups", "req", "pair"), "head"),
            P(("groups", "req", "pair"), "head"),
            P(("groups", "req", "pair"), "head"),
            P(("groups", "req", "pair"), None, "head"),
            P(("groups", "req", "pair"), None, "head"),
            P(("groups", "req", "pair")),
            P(("groups", "req", "pair"), "head"),
            P("head"),
            P(("req", "pair"), "head"),
            P(("req", "pair"), "head"),
            P(("req", "pair"), "head"),
        ),
        out_specs=P(("groups", "req", "pair"), "head"),
        check_vma=False,
    )
```
